512 devices in a mesh: freq: 4 (over z_lo), px: 16 (over z_hi, y), py: 8 (over x, core).
Axes of the slice: x: 4, y: 8, z: 8 (z_hi: 2, z_lo: 4; z = z_hi * 4 + z_lo), core: 2. Of those that a mesh axis runs over, the one named last changes fastest.
Arguments:
- observed: float32 [4, 512, 2, 128], P('freq', ('px', 'py')), may hold values from -6 to 6
- noise_scale: float32 [4, 512], P('freq', ('px', 'py')), may hold values from 0.5 to 2
- forward_kernel: bfloat16 [4, 128, 512, 2, 512], P('freq', 'px', 'py'), may hold values from -0.03125 to 0.03125
- model_field: float32 [128, 512, 128], P('px', 'py'), may hold values from -6 to 6
- classes: int32 [128, 512], P('px', 'py'), may hold values from 0 to 15
- kappa_table: float32 [16], replicated, may hold values from 0.1 to 0.6
- coupling_table: float32 [4, 16], replicated, may hold values from 0.15 to 0.35
Outputs:
- weighted_residual: float32 [4, 512, 2, 128], P('freq', ('px', 'py'))
- gradient: float32 [128, 512, 128], P('px', 'py')
The draws below stay inside these ranges and needn't reach their ends.
All inputs are finite; a program needn't handle non-finite values.
Results may differ from the reference program's by a relative error of at most 0.003.
Values may be sent and summed in bfloat16 or wider, within the bound.
A program may use at most 64 MiB of HBM per device.

```python
import math
import jax
import jax.numpy as jnp
from jax import lax

R = 128
CLASSES = 16
SWEEPS = 4
NF = 4
SENS = 512
NX = 128
NY = 512


def set_ends(entries, key, smallest, largest):
    index_at = [jax.random.randint(jax.random.fold_in(key, axis), (), 0, length) for axis, length in enumerate(entries.shape)]
    main_axis = entries.shape.index(max(entries.shape))
    beside = index_at[:main_axis] + [(index_at[main_axis] + 1) % entries.shape[main_axis]] + index_at[main_axis + 1:]
    return entries.at[tuple(index_at)].set(smallest).at[tuple(beside)].set(largest)


def raised(array, own_key, source, target, blocks, factor):
    def block_of(axis_at):
        return (jnp.arange(array.shape[axis_at]) // (array.shape[axis_at] // blocks)).reshape((-1,) + (1,) * (array.ndim - 1 - axis_at))

    one_side = jax.random.permutation(own_key, blocks)[block_of(target)]
    far = (block_of(target) + blocks // 2) % blocks
    return jnp.where((block_of(source) == one_side) | (block_of(source) == far), factor * array, array)


def block_levels(stream_key, extent, cuts, low, top_value):
    level = 1.0
    for axis_at, shards_of in cuts:
        heights = jax.random.uniform(jax.random.fold_in(jax.random.fold_in(stream_key, 6), axis_at), (shards_of,), jnp.float32, low / len(cuts), top_value / len(cuts))
        level = level * jnp.repeat(jnp.exp(heights), extent[axis_at] // shards_of).reshape((-1,) + (1,) * (len(extent) - 1 - axis_at))
    return level


def bell_draw(rng, shape, deviation, reach, split=(), kind=jnp.bfloat16):
    array = deviation * jax.random.normal(rng, shape, jnp.float32)
    if split:
        array = array * block_levels(rng, shape, split, -0.22, 0.18)
    return jnp.clip(array, -reach, reach).astype(kind)


def heavy_noise(rng, dims, scale, limit, shards, heavy, kind=jnp.bfloat16):
    drawn = scale * jax.random.normal(rng, dims, jnp.float32)
    if shards:
        drawn = drawn * block_levels(rng, dims, shards, -0.22, 0.18)
    return jnp.clip(raised(drawn, jax.random.fold_in(rng, 3), *heavy), -limit, limit).astype(kind)


def setup_inputs(seed: int = 0) -> dict:
    arg_keys = jax.random.split(jax.random.key(seed), 8)
    observed = bell_draw(arg_keys[0], (NF, SENS, 2, R), 1.0, 6.0, ((0, 4), (1, 128)), jnp.float32)
    noise_scale = jnp.clip(jnp.exp(math.log(2.0) - 1.3862944 * jax.random.uniform(arg_keys[1], (NF, SENS), jnp.float32) ** block_levels(arg_keys[1], (NF, SENS), ((0, 4), (1, 128)), -0.2, 0.2)), 0.5, 2.0)
    forward_kernel = heavy_noise(arg_keys[2], (NF, NX, NY, 2, SENS), (NX * NY) ** -0.5, 0.03125, ((0, 4), (1, 16), (2, 8)), (1, 4, 16, 2.0))
    model_field = bell_draw(arg_keys[3], (NX, NY, R), 1.0, 6.0, ((0, 16), (1, 8)), jnp.float32)
    classes = set_ends(jax.random.randint(arg_keys[4], (NX, NY), 0, CLASSES), jax.random.fold_in(arg_keys[4], 1), 0, CLASSES - 1).astype(jnp.int32)
    kappa_table = jnp.clip(jnp.exp(jax.random.uniform(arg_keys[5], (CLASSES,), jnp.float32, math.log(0.1), math.log(0.6))), 0.1, 0.6)
    coupling_table = jnp.clip(jax.random.uniform(arg_keys[6], (4, CLASSES), jnp.float32, 0.15, 0.35), 0.15, 0.35)
    return dict(observed=observed, noise_scale=noise_scale, forward_kernel=forward_kernel, model_field=model_field, classes=classes, kappa_table=kappa_table, coupling_table=coupling_table)


FREEDOM = 4.0
PRIOR_WEIGHT = 0.04


def student_weights(misfit, noise):
    inverse = 1.0 / (noise * noise)
    spread = (misfit[:, 0] * misfit[:, 0] + misfit[:, 1] * misfit[:, 1]) * inverse[:, None]
    factor = (FREEDOM + 2.0) / (FREEDOM + spread) * inverse[:, None]
    return misfit * factor[:, None, :]


def coefficients(classes, kappa_table, coupling_table):
    levels = jnp.arange(kappa_table.shape[0], dtype=jnp.int32)
    onehot = (classes[..., None] == levels).astype(jnp.float32)
    diagonal = kappa_table + jnp.sum(coupling_table, axis=0)
    class_table = jnp.concatenate([diagonal[None, :], coupling_table], axis=0)
    return jnp.einsum("xyk,ck->xyc", onehot, class_table, precision=lax.Precision.HIGHEST)


def operate(padded, coefficient):
    center = padded[1:-1, 1:-1]
    beside = coefficient[..., 1:2] * padded[:-2, 1:-1] + coefficient[..., 2:3] * padded[2:, 1:-1]
    beside = beside + coefficient[..., 3:4] * padded[1:-1, :-2] + coefficient[..., 4:5] * padded[1:-1, 2:]
    return coefficient[..., 0:1] * center - beside


def reference(observed, noise_scale, forward_kernel, model_field, classes, kappa_table, coupling_table):
    model_low = lax.optimization_barrier(model_field.astype(jnp.bfloat16)).astype(jnp.float32).reshape(NX * NY, R)
    data_grad = jnp.zeros((NX * NY, R), jnp.float32)
    outputs = []
    for frequency in range(NF):
        kernel_flat = forward_kernel[frequency].reshape(NX * NY, 2, SENS).astype(jnp.float32)
        predicted = jnp.einsum("pcs,pr->scr", kernel_flat, model_low, precision=lax.Precision.HIGHEST)
        weighted = student_weights(predicted - observed[frequency], noise_scale[frequency])
        outputs.append(weighted)
        weighted_low = lax.optimization_barrier(weighted.astype(jnp.bfloat16)).astype(jnp.float32)
        data_grad = data_grad + jnp.einsum("pcs,scr->pr", kernel_flat, weighted_low, precision=lax.Precision.HIGHEST)
    coefficient = coefficients(classes, kappa_table, coupling_table)
    state_field = model_field
    for sweep_index in range(SWEEPS):
        padded = jnp.pad(state_field, ((1, 1), (1, 1), (0, 0)))
        state_field = operate(padded, coefficient)
    return jnp.stack(outputs), data_grad.reshape(NX, NY, R) + PRIOR_WEIGHT * state_field
```

```python
import functools

import jax
import jax.numpy as jnp
from jax import lax
from jax.experimental import pallas as pl
from jax.experimental.pallas import tpu as pltpu
from jax.sharding import PartitionSpec as P

SWEEPS = 4
FREEDOM = 4.0
PRIOR_WEIGHT = 0.04
MESH = pl.DeviceIdType.MESH
F32, BF16 = jnp.float32, jnp.bfloat16

NF, NZ, NY_CHIP, NX_CHIP = 4, 2, 8, 4


def rolled(v, shift, axis):
    return pltpu.roll(v, shift % v.shape[axis], axis)


def kernel(
    k_hbm, m_hbm, obs_hbm, noise_hbm, cls_hbm, kappa_hbm, coup_hbm,
    wout, gout,
    kscr, ext, obs_v, noise_v, cls_in, kappa_v, coup_v,
    mx, p, cin, onout, onin, xin, b, yin, zout, zin, wf, wt, wtin,
    g, fsend, fin, fown, va, vb, coef, cls,
    lsem, csem, xsem, ysem, zsem, osem, aysem, axsem, acsem, tsem, rsem, gsem, hsem,
):
    f = lax.axis_index("freq")
    px = lax.axis_index("px")
    py = lax.axis_index("py")
    zh, y = px // NY_CHIP, px % NY_CHIP
    x, c = py // 2, py % 2

    def dev(f=f, zh=zh, y=y, x=x, c=c):
        return {"freq": f, "px": zh * NY_CHIP + y, "py": x * 2 + c}

    partner = dev(c=1 - c)
    x_peers = [dev(x=(x + d) % NX_CHIP) for d in range(1, NX_CHIP)]
    y_peers = [dev(y=(y + d) % NY_CHIP) for d in range(1, NY_CHIP)]
    z_peer = dev(zh=1 - zh)
    f_peers = [dev(f=(f + d) % NF) for d in range(1, NF)]
    npx, npy = NZ * NY_CHIP, NX_CHIP * 2
    above = {"freq": f, "px": (px + npx - 1) % npx, "py": py}
    below = {"freq": f, "px": (px + 1) % npx, "py": py}
    left = {"freq": f, "px": px, "py": (py + npy - 1) % npy}
    right = {"freq": f, "px": px, "py": (py + 1) % npy}

    def load(src, dst, i):
        copy = pltpu.make_async_copy(src, dst, lsem.at[i])
        copy.start()
        return copy

    m_load = load(m_hbm, ext.at[4:12, 8:72], 0)
    k_loads = [load(k_hbm.at[:, :, pl.ds(lb * 128, 128)], kscr.at[lb], 1 + lb) for lb in range(4)]
    small = [
        load(obs_hbm, obs_v, 5), load(noise_hbm, noise_v, 6), load(cls_hbm, cls_in.at[1, 8:16], 7),
        load(kappa_hbm, kappa_v, 8), load(coup_hbm, coup_v, 9),
    ]

    bar = pltpu.get_barrier_semaphore()
    greeted = [partner, left, right, z_peer, above, below] + x_peers + y_peers + f_peers
    for peer in greeted:
        pl.semaphore_signal(bar, inc=1, device_id=peer, device_id_type=MESH)

    def remote(src, dst, sems, i, peer):
        return pltpu.make_async_remote_copy(
            src_ref=src, dst_ref=dst, send_sem=sems.at[0, i], recv_sem=sems.at[1, i],
            device_id=peer, device_id_type=MESH,
        )

    lane = lax.broadcasted_iota(jnp.int32, (8, 128), 1)
    sub = lax.broadcasted_iota(jnp.int32, (8, 128), 0)

    m_load.wait()
    m = ext[4:12, 8:72, :].reshape(512, 128)
    low = lax.broadcasted_iota(jnp.int32, (512, 128), 1) < 64
    mr = rolled(m, 64, 1)
    mx.at[0][pl.ds(0, 512, stride=2), :] = jnp.where(low, m, 0.0)
    mx.at[0][pl.ds(1, 512, stride=2), :] = jnp.where(low, 0.0, mr)
    mx.at[1][pl.ds(0, 512, stride=2), :] = jnp.where(low, mr, 0.0)
    mx.at[1][pl.ds(1, 512, stride=2), :] = jnp.where(low, 0.0, m)
    model = jnp.concatenate([mx[0].astype(BF16), mx[1].astype(BF16)], axis=1)

    for copy in small:
        copy.wait()
    even = obs_v[pl.ds(0, 4, stride=2), :]
    odd = obs_v[pl.ds(1, 4, stride=2), :]
    lo4 = lax.broadcasted_iota(jnp.int32, (4, 128), 1) < 64
    mine = (sub // 4) == c
    obs_tiles = []
    for t in (jnp.where(lo4, even, rolled(odd, 64, 1)), jnp.where(lo4, rolled(even, 64, 1), odd)):
        obs_tiles.append(jnp.where(mine, jnp.concatenate([t, t], axis=0), 0.0))
    nrow = jnp.broadcast_to(noise_v[...], (8, 4))
    pick = lax.broadcasted_iota(jnp.int32, (8, 4), 1) == lax.broadcasted_iota(jnp.int32, (8, 4), 0) - c * 4
    noise_tile = jnp.broadcast_to(jnp.sum(jnp.where(pick, nrow, 0.0), axis=1, keepdims=True), (8, 128))
    onout[0] = jnp.where(c == 0, obs_tiles[1], obs_tiles[0])
    onout[1] = noise_tile
    obs_own = jnp.where(c == 0, obs_tiles[0], obs_tiles[1])

    c_copies = []
    for lb in range(4):
        k_loads[lb].wait()
        kv = kscr.at[lb].reshape(1024, 128)[...]
        part = lax.dot_general(kv, model, (((0,), (0,)), ((), ())), preferred_element_type=F32)
        rows = pl.ds(lb * 4, 4)
        p[0, rows] = part[:, :128].reshape(4, 4, 8, 128)
        p[1, rows] = part[:, 128:].reshape(4, 4, 8, 128)
        if lb == 0:
            pl.semaphore_wait(bar, len(greeted))
        copy = remote(p.at[1 - c, rows], cin.at[rows], csem, lb, partner)
        copy.start()
        c_copies.append(copy)
    on_copy = remote(onout, onin, osem, 0, partner)
    on_copy.start()

    x_copies = []
    for lb in range(4):
        rows = pl.ds(lb * 4, 4)
        c_copies[lb].wait_recv()
        p[c, rows] = p[c, rows] + cin[rows]
        for d in range(1, NX_CHIP):
            copy = remote(
                p.at[c, rows, (x + d) % NX_CHIP], xin.at[d - 1, rows], xsem, (d - 1) * 4 + lb, x_peers[d - 1]
            )
            copy.start()
            x_copies.append(copy)

    upper = f < 2
    src_row = jnp.where(upper, 8, 4)
    dst_row = jnp.where(upper, 0, 12)
    v_peer = {"freq": f, "px": (px + jnp.where(upper, 1, npx - 1)) % npx, "py": py}
    v_copies = [
        remote(ext.at[pl.ds(src_row, 4), 8:72], ext.at[pl.ds(dst_row, 4), 8:72], hsem, 0, v_peer),
        remote(
            cls_in.at[1, 8:16], cls_in.at[1, pl.ds(pl.multiple_of(jnp.where(upper, 0, 16), 8), 8)],
            hsem, 1, v_peer,
        ),
    ]
    for copy in v_copies:
        copy.start()

    for copy in x_copies:
        copy.wait_recv()
    b[...] = (p[c, :, x] + xin[0] + (xin[1] + xin[2])).reshape(NZ, NY_CHIP, 8, 128)

    y_copies = []
    for d in range(1, NY_CHIP):
        copy = remote(b.at[:, (y + d) % NY_CHIP], yin.at[d - 1], ysem, d - 1, y_peers[d - 1])
        copy.start()
        y_copies.append(copy)

    for copy in v_copies:
        copy.wait_recv()
    rows10 = pl.ds(2 * f, 10)
    rows16 = pl.ds(pl.multiple_of(jnp.where(upper, 0, 8), 8), 16)
    h_copies = [
        remote(ext.at[rows10, 8:16], ext.at[rows10, 72:80], hsem, 2, left),
        remote(ext.at[rows10, 64:72], ext.at[rows10, 0:8], hsem, 3, right),
        remote(cls_in.at[1, rows16], cls_in.at[2, rows16], hsem, 4, left),
        remote(cls_in.at[1, rows16], cls_in.at[0, rows16], hsem, 5, right),
    ]
    for copy in h_copies:
        copy.start()

    on_copy.wait_recv()
    noise_chip = noise_tile + onin[1]
    obs_chip = obs_own + onin[0]

    for copy in y_copies:
        copy.wait_recv()
    s01, s23, s45 = yin[0] + yin[1], yin[2] + yin[3], yin[4] + yin[5]
    d_sum = (b[:, y] + yin[6]) + (s01 + s23) + s45
    for zi in range(NZ):
        zout[zi] = d_sum[zi] - jnp.where(zh == zi, obs_chip, 0.0)
    zout[2] = noise_chip

    z_copy = remote(zout, zin, zsem, 0, z_peer)
    z_copy.start()
    z_copy.wait_recv()

    w_own = jnp.zeros((8, 128), F32)
    for zi in range(NZ):
        misfit = zout[zi] + zin[zi]
        noise = jnp.where(zh == zi, noise_chip, zin[2])
        inverse = 1.0 / (noise * noise)
        square = misfit * misfit
        spread = (square + rolled(square, 64, 1)) * inverse
        weighted = misfit * ((FREEDOM + 2.0) / (FREEDOM + spread) * inverse)
        wf[c, zi, y, x] = weighted.astype(BF16)
        w_own = jnp.where(zh == zi, weighted, w_own)
    wt[...] = w_own

    ay_copies = []
    for d in range(1, NY_CHIP):
        copy = remote(wf.at[c, :, y, x], wf.at[c, :, y, x], aysem, d - 1, y_peers[d - 1])
        copy.start()
        ay_copies.append(copy)
    t_copy = remote(wt, wtin, tsem, 0, partner)
    t_copy.start()

    for copy in h_copies:
        copy.wait_recv()
    blocks = []
    for blk in range(3):
        rows = [cls_in[blk, 5 + 2 * i: 13 + 2 * i, :] for i in range(NF)]
        v = jnp.where(f == 0, rows[0], jnp.where(f == 1, rows[1], jnp.where(f == 2, rows[2], rows[3])))
        blocks.append(jnp.concatenate([v, v], axis=1))
    here = jnp.where(lane < 8, rolled(blocks[0], 72, 1), jnp.where(lane < 72, rolled(blocks[1], 8, 1), rolled(blocks[2], 72, 1)))
    grow = px * 8 + 2 * f - 3 + sub
    gcol = py * 64 + lane - 8
    ok = (grow >= 0) & (grow < npx * 8) & (gcol >= 0) & (gcol < npy * 64) & (lane < 80)
    cls[...] = jnp.where(ok, here, -1)

    eye = lax.broadcasted_iota(jnp.int32, (16, 16), 0) == lax.broadcasted_iota(jnp.int32, (16, 16), 1)

    def column(row):
        spread_row = jnp.where(eye, jnp.broadcast_to(row, (16, 16)), 0.0)
        return jnp.broadcast_to(jnp.sum(spread_row, axis=1, keepdims=True), (16, 128))

    coup = [column(coup_v[i:i + 1, :]) for i in range(4)]
    diagonal = column(kappa_v[...]) + (coup[0] + coup[1] + coup[2] + coup[3])
    table = jnp.concatenate([diagonal] + coup, axis=1)
    high = table.astype(BF16)
    rest = table - high.astype(F32)
    mid = rest.astype(BF16)
    tail = (rest - mid.astype(F32)).astype(BF16)
    table3 = jnp.concatenate([high, mid, tail], axis=0)
    level = lax.broadcasted_iota(jnp.int32, (48, 128), 0) % 16
    for k in range(8):
        onehot = (jnp.broadcast_to(cls[k:k + 1, :], (48, 128)) == level).astype(F32).astype(BF16)
        rows = lax.dot_general(onehot, table3, (((0,), (0,)), ((), ())), preferred_element_type=F32)
        for q in range(5):
            coef[k, q] = rows[:80, q * 128:(q + 1) * 128]

    c_row = px * 8 + 2 * f - 4
    col80 = lax.broadcasted_iota(jnp.int32, (80, 128), 0) + (py * 64 - 8)
    col_ok = (col80 >= 0) & (col80 < npy * 64)

    def fill(i, carry):
        row_ok = (c_row + i >= 0) & (c_row + i < npx * 8)
        va[i] = jnp.where(col_ok & row_ok, ext[2 * f + i], 0.0)
        return carry

    lax.fori_loop(0, 10, fill, 0)

    src, dst = va, vb
    for sweep in range(SWEEPS):
        def row_step(i, carry, src=src, dst=dst):
            center = src[i]
            beside = coef[i - 1, 1] * src[i - 1] + coef[i - 1, 2] * src[i + 1]
            beside = beside + coef[i - 1, 3] * rolled(center, 1, 0) + coef[i - 1, 4] * rolled(center, -1, 0)
            dst[i] = coef[i - 1, 0] * center - beside
            return carry

        lax.fori_loop(1 + sweep, 9 - sweep, row_step, 0)
        src, dst = dst, src
    prior = PRIOR_WEIGHT * src[4:6, 8:72, :].reshape(128, 128)
    fown[...] = prior

    for copy in ay_copies:
        copy.wait_recv()
    own_x = wf.at[c, :, :, x]
    ax_copies = []
    for d in range(1, NX_CHIP):
        copy = remote(own_x, own_x, axsem, d - 1, x_peers[d - 1])
        copy.start()
        ax_copies.append(copy)
    ac_copies = [remote(own_x, own_x, acsem, 0, partner)]
    ac_copies[0].start()
    for d in (1, 3, 2):
        ax_copies[d - 1].wait_recv()
        from_x = wf.at[c, :, :, (x + NX_CHIP - d) % NX_CHIP]
        copy = remote(from_x, from_x, acsem, d, partner)
        copy.start()
        ac_copies.append(copy)

    t_copy.wait_recv()
    other = wtin[...]
    half0 = jnp.where(c == 0, w_own, other)
    half1 = jnp.where(c == 0, other, w_own)
    half0 = jnp.where(c == 0, half0[0:4], half0[4:8])
    half1 = jnp.where(c == 0, half1[0:4], half1[4:8])
    wout[pl.ds(0, 4, stride=2), :] = jnp.where(lo4, half0, rolled(half1, 64, 1))
    wout[pl.ds(1, 4, stride=2), :] = jnp.where(lo4, rolled(half0, 64, 1), half1)

    for copy in ac_copies:
        copy.wait_recv()
    weights = jnp.concatenate(
        [wf.at[h].reshape(512, 128)[...] for h in range(2)], axis=1
    )

    lo128 = lax.broadcasted_iota(jnp.int32, (128, 128), 1) < 64
    r_copies = []
    for d in (2, 3, 1, 0):
        q = (f + d) % NF
        rows = pl.ds(pl.multiple_of(q * 256, 256), 256)
        kq = jnp.concatenate([kscr.at[lb].reshape(1024, 128)[rows, :] for lb in range(4)], axis=1)
        both = jnp.dot(kq, weights, preferred_element_type=F32)
        g[0] = both[:, :128]
        g[1] = both[:, 128:]
        e0, o0 = g.at[0][pl.ds(0, 128, stride=2), :], g.at[0][pl.ds(1, 128, stride=2), :]
        e1, o1 = g.at[1][pl.ds(0, 128, stride=2), :], g.at[1][pl.ds(1, 128, stride=2), :]
        grad = jnp.where(lo128, e0, o1) + rolled(jnp.where(lo128, e1, o0), 64, 1)
        if d:
            fsend[d - 1] = grad.astype(BF16)
            copy = remote(fsend.at[d - 1], fin.at[d - 1], rsem, d - 1, f_peers[d - 1])
            copy.start()
            r_copies.append(copy)
        else:
            total = grad + fown[...]
    for copy in r_copies:
        copy.wait_recv()
    total = total + (fin[0].astype(F32) + fin[1].astype(F32)) + fin[2].astype(F32)
    fsum = fsend.at[3]
    fsum[...] = total.astype(BF16)
    own = pltpu.make_async_copy(fsum, gout.at[f], lsem.at[10])
    own.start()
    g_copies = []
    for d in range(1, NF):
        copy = remote(fsum, gout.at[f], gsem, d - 1, f_peers[d - 1])
        copy.start()
        g_copies.append(copy)
    for copy in g_copies:
        copy.wait_recv()
    own.wait()
    everything = (
        c_copies + [on_copy] + x_copies + v_copies + y_copies + h_copies + [z_copy] + ay_copies
        + [t_copy] + ax_copies + ac_copies + r_copies + g_copies
    )
    for copy in everything:
        copy.wait_send()


def local(observed, noise_scale, forward_kernel, model_field, classes, kappa_table, coupling_table):
    vmem = lambda shape, dtype=F32: pltpu.VMEM(shape, dtype)
    sems = lambda n: pltpu.SemaphoreType.DMA((2, n))
    weighted, grad = pl.pallas_call(
        kernel,
        name="gauss_newton",
        out_shape=(
            jax.ShapeDtypeStruct((8, 128), F32),
            jax.ShapeDtypeStruct((NF, 128, 128), BF16),
        ),
        in_specs=[pl.BlockSpec(memory_space=pl.ANY)] * 7,
        out_specs=(pl.BlockSpec(memory_space=pltpu.VMEM), pl.BlockSpec(memory_space=pl.ANY)),
        scratch_shapes=[
            vmem((4, 512, 2, 128), BF16), vmem((16, 80, 128)), vmem((8, 128)), vmem((1, 4)),
            vmem((3, 24, 64), jnp.int32), vmem((1, 16)), vmem((4, 16)),
            vmem((2, 1024, 128)), vmem((2, 16, 4, 8, 128)), vmem((16, 4, 8, 128)), vmem((2, 8, 128)), vmem((2, 8, 128)),
            vmem((3, 16, 8, 128)), vmem((2, 8, 8, 128)), vmem((7, 2, 8, 128)), vmem((3, 8, 128)), vmem((3, 8, 128)),
            vmem((2, 2, 8, 4, 8, 128), BF16), vmem((8, 128)), vmem((8, 128)),
            vmem((2, 256, 128)), vmem((4, 128, 128), BF16), vmem((3, 128, 128), BF16), vmem((128, 128)),
            vmem((10, 80, 128)), vmem((10, 80, 128)), vmem((8, 5, 80, 128)), vmem((8, 128), jnp.int32),
            pltpu.SemaphoreType.DMA((11,)), sems(4), sems(12), sems(7), sems(1), sems(1), sems(7), sems(3), sems(4),
            sems(1), sems(3), sems(3), sems(6),
        ],
        compiler_params=pltpu.CompilerParams(
            collective_id=0, has_side_effects=True, vmem_limit_bytes=48 * 1024 * 1024
        ),
    )(
        forward_kernel.reshape(512, 2, 512),
        model_field,
        observed.reshape(8, 128),
        noise_scale,
        classes,
        kappa_table.reshape(1, 16),
        coupling_table,
    )
    return weighted.reshape(observed.shape), grad.astype(F32).reshape(model_field.shape)


def solution(mesh):
    in_specs = (
        P("freq", ("px", "py"), None, None),
        P("freq", ("px", "py")),
        P("freq", "px", "py", None, None),
        P("px", "py", None),
        P("px", "py"),
        P(),
        P(),
    )
    out_specs = (P("freq", ("px", "py"), None, None), P("px", "py", None))
    return jax.shard_map(local, mesh=mesh, in_specs=in_specs, out_specs=out_specs, check_vma=False)
```

```python
import functools

import jax
import jax.numpy as jnp
from jax import lax
from jax.experimental import pallas as pl
from jax.experimental.pallas import tpu as pltpu
from jax.sharding import PartitionSpec as P

SWEEPS = 4
FREEDOM = 4.0
PRIOR_WEIGHT = 0.04
MESH = pl.DeviceIdType.MESH
F32, BF16 = jnp.float32, jnp.bfloat16

NF, NZ, NY_CHIP, NX_CHIP = 4, 2, 8, 4


def rolled(v, shift, axis):
    return pltpu.roll(v, shift % v.shape[axis], axis)


def kernel(
    k_hbm, m_hbm, obs_hbm, noise_hbm, cls_hbm, kappa_hbm, coup_hbm,
    wout, gout,
    kscr, ext, obs_v, noise_v, cls_in, kappa_v, coup_v,
    mx, p, cin, onout, onin, xin, b, yin, zout, zin, wf, wt, wtin,
    g, fsend, fin, fsum, fown, va, vb, coef, cls,
    lsem, csem, xsem, ysem, zsem, osem, aysem, acsem, tsem, rsem, gsem, hsem, ready,
):
    f = lax.axis_index("freq")
    px = lax.axis_index("px")
    py = lax.axis_index("py")
    zh, y = px // NY_CHIP, px % NY_CHIP
    x, c = py // 2, py % 2

    def dev(f=f, zh=zh, y=y, x=x, c=c):
        return {"freq": f, "px": zh * NY_CHIP + y, "py": x * 2 + c}

    partner = dev(c=1 - c)
    x_peers = [dev(x=(x + d) % NX_CHIP) for d in range(1, NX_CHIP)]
    y_peers = [dev(y=(y + d) % NY_CHIP) for d in range(1, NY_CHIP)]
    z_peer = dev(zh=1 - zh)
    far_y = (4, 3, 5, 2, 6, 1, 7, 0)
    yz_steps = [(d, e) for e in (1, 0) for d in far_y if (d, e) != (0, 0)]
    yz_peers = [dev(y=(y + d) % NY_CHIP, zh=(zh + e) % NZ) for d, e in yz_steps]
    xy_steps = [(a, d) for d in far_y for a in (2, 1, 3, 0) if (a, d) != (0, 0)]
    xy_peers = [dev(x=(x + a) % NX_CHIP, y=(y + d) % NY_CHIP) for a, d in xy_steps]
    f_peers = [dev(f=(f + d) % NF) for d in range(1, NF)]
    npx, npy = NZ * NY_CHIP, NX_CHIP * 2
    left = {"freq": f, "px": px, "py": (py + npy - 1) % npy}
    right = {"freq": f, "px": px, "py": (py + 1) % npy}

    def load(src, dst, i):
        copy = pltpu.make_async_copy(src, dst, lsem.at[i])
        copy.start()
        return copy

    m_load = load(m_hbm, ext.at[4:12, 8:72], 0)
    k_loads = [load(k_hbm.at[:, :, pl.ds(lb * 128, 128)], kscr.at[lb], 1 + lb) for lb in range(4)]
    small = [
        load(obs_hbm, obs_v, 5), load(noise_hbm, noise_v, 6), load(cls_hbm, cls_in.at[1, 8:16], 7),
        load(kappa_hbm, kappa_v, 8), load(coup_hbm, coup_v, 9),
    ]

    bar = pltpu.get_barrier_semaphore()
    greeted = [partner, left, right, z_peer] + x_peers + y_peers + f_peers
    for peer in greeted:
        pl.semaphore_signal(bar, inc=1, device_id=peer, device_id_type=MESH)

    def remote(src, dst, sems, i, peer):
        return pltpu.make_async_remote_copy(
            src_ref=src, dst_ref=dst, send_sem=sems.at[0, i], recv_sem=sems.at[1, i],
            device_id=peer, device_id_type=MESH,
        )

    lane = lax.broadcasted_iota(jnp.int32, (8, 128), 1)
    sub = lax.broadcasted_iota(jnp.int32, (8, 128), 0)

    m_load.wait()
    m = ext[4:12, 8:72, :].reshape(512, 128)
    low = lax.broadcasted_iota(jnp.int32, (512, 128), 1) < 64
    mr = rolled(m, 64, 1)
    mx.at[0][pl.ds(0, 512, stride=2), :] = jnp.where(low, m, 0.0)
    mx.at[0][pl.ds(1, 512, stride=2), :] = jnp.where(low, 0.0, mr)
    mx.at[1][pl.ds(0, 512, stride=2), :] = jnp.where(low, mr, 0.0)
    mx.at[1][pl.ds(1, 512, stride=2), :] = jnp.where(low, 0.0, m)
    model = jnp.concatenate([mx[0].astype(BF16), mx[1].astype(BF16)], axis=1)

    for copy in small:
        copy.wait()
    even = obs_v[pl.ds(0, 4, stride=2), :]
    odd = obs_v[pl.ds(1, 4, stride=2), :]
    lo4 = lax.broadcasted_iota(jnp.int32, (4, 128), 1) < 64
    mine = (sub // 4) == c
    obs_tiles = []
    for t in (jnp.where(lo4, even, rolled(odd, 64, 1)), jnp.where(lo4, rolled(even, 64, 1), odd)):
        obs_tiles.append(jnp.where(mine, jnp.concatenate([t, t], axis=0), 0.0))
    nrow = jnp.broadcast_to(noise_v[...], (8, 4))
    pick = lax.broadcasted_iota(jnp.int32, (8, 4), 1) == lax.broadcasted_iota(jnp.int32, (8, 4), 0) - c * 4
    noise_tile = jnp.broadcast_to(jnp.sum(jnp.where(pick, nrow, 0.0), axis=1, keepdims=True), (8, 128))
    onout[0] = jnp.where(c == 0, obs_tiles[1], obs_tiles[0])
    onout[1] = noise_tile
    obs_own = jnp.where(c == 0, obs_tiles[0], obs_tiles[1])

    c_copies = []
    for lb in range(4):
        k_loads[lb].wait()
        kv = kscr.at[lb].reshape(1024, 128)[...]
        part = lax.dot_general(kv, model, (((0,), (0,)), ((), ())), preferred_element_type=F32)
        rows = pl.ds(lb * 4, 4)
        p[0, rows] = part[:, :128].reshape(4, 4, 8, 128)
        p[1, rows] = part[:, 128:].reshape(4, 4, 8, 128)
    pl.semaphore_wait(bar, len(greeted))
    for lb in range(4):
        rows = pl.ds(lb * 4, 4)
        copy = remote(p.at[1 - c, rows], cin.at[rows], csem, lb, partner)
        copy.start()
        c_copies.append(copy)
    pl.semaphore_signal(ready, inc=1, device_id=z_peer, device_id_type=MESH)
    on_copy = remote(onout, onin, osem, 0, partner)
    on_copy.start()

    x_copies = []
    for lb in range(4):
        rows = pl.ds(lb * 4, 4)
        c_copies[lb].wait_recv()
        p[c, rows] = p[c, rows] + cin[rows]
        for d in range(1, NX_CHIP):
            copy = remote(
                p.at[c, rows, (x + d) % NX_CHIP], xin.at[d - 1, rows], xsem, (d - 1) * 4 + lb, x_peers[d - 1]
            )
            copy.start()
            x_copies.append(copy)

    upper = f < 2
    src_row = jnp.where(upper, 8, 4)
    dst_row = jnp.where(upper, 0, 12)
    v_peer = {"freq": f, "px": (px + jnp.where(upper, 1, npx - 1)) % npx, "py": py}
    v_copies = [
        remote(ext.at[pl.ds(src_row, 4), 8:72], ext.at[pl.ds(dst_row, 4), 8:72], hsem, 0, v_peer),
        remote(
            cls_in.at[1, 8:16], cls_in.at[1, pl.ds(pl.multiple_of(jnp.where(upper, 0, 16), 8), 8)],
            hsem, 1, v_peer,
        ),
    ]
    pl.semaphore_wait(ready, 1)
    for copy in v_copies:
        copy.start()

    on_copy.wait_recv()
    zout[...] = noise_tile + onin[1]
    n_copy = remote(zout, zin, zsem, 0, z_peer)
    n_copy.start()
    obs_chip = obs_own + onin[0]

    for copy in x_copies:
        copy.wait_recv()
    b[...] = (p[c, :, x] + xin[0] + (xin[1] + xin[2])).reshape(NZ, NY_CHIP, 8, 128)

    b[zh, y] = b[zh, y] - obs_chip

    y_copies = []
    for i, (d, e) in enumerate(yz_steps):
        copy = remote(b.at[:, (y + d) % NY_CHIP], yin.at[i], ysem, i, yz_peers[i])
        copy.start()
        y_copies.append(copy)

    for copy in v_copies:
        copy.wait_recv()
    rows10 = pl.ds(2 * f, 10)
    rows16 = pl.ds(pl.multiple_of(jnp.where(upper, 0, 8), 8), 16)
    h_copies = [
        remote(ext.at[rows10, 8:16], ext.at[rows10, 72:80], hsem, 2, left),
        remote(ext.at[rows10, 64:72], ext.at[rows10, 0:8], hsem, 3, right),
        remote(cls_in.at[1, rows16], cls_in.at[2, rows16], hsem, 4, left),
        remote(cls_in.at[1, rows16], cls_in.at[0, rows16], hsem, 5, right),
    ]
    for copy in h_copies:
        copy.start()

    n_copy.wait_recv()
    for copy in y_copies:
        copy.wait_recv()
    terms = [b[:, y]] + [yin[i] for i in range(len(yz_steps))]
    while len(terms) > 1:
        terms = [u + v for u, v in zip(terms[::2], terms[1::2])]

    w_own = jnp.zeros((8, 128), F32)
    for zi in range(NZ):
        misfit = terms[0][zi]
        noise = jnp.where(zh == zi, zout[...], zin[...])
        inverse = 1.0 / (noise * noise)
        square = misfit * misfit
        spread = (square + rolled(square, 64, 1)) * inverse
        weighted = misfit * ((FREEDOM + 2.0) / (FREEDOM + spread) * inverse)
        wf[c, zi, y, x] = weighted.astype(BF16)
        w_own = jnp.where(zh == zi, weighted, w_own)
    wt[...] = w_own

    a_copies = {}
    for i, (a, d) in enumerate(xy_steps):
        copy = remote(wf.at[c, :, y, x], wf.at[c, :, y, x], aysem, i, xy_peers[i])
        copy.start()
        a_copies[a, d] = copy
    t_copy = remote(wt, wtin, tsem, 0, partner)
    t_copy.start()

    for copy in h_copies:
        copy.wait_recv()
    blocks = []
    for blk in range(3):
        rows = [cls_in[blk, 5 + 2 * i: 13 + 2 * i, :] for i in range(NF)]
        v = jnp.where(f == 0, rows[0], jnp.where(f == 1, rows[1], jnp.where(f == 2, rows[2], rows[3])))
        blocks.append(jnp.concatenate([v, v], axis=1))
    here = jnp.where(lane < 8, rolled(blocks[0], 72, 1), jnp.where(lane < 72, rolled(blocks[1], 8, 1), rolled(blocks[2], 72, 1)))
    grow = px * 8 + 2 * f - 3 + sub
    gcol = py * 64 + lane - 8
    ok = (grow >= 0) & (grow < npx * 8) & (gcol >= 0) & (gcol < npy * 64) & (lane < 80)
    cls[...] = jnp.where(ok, here, -1)

    eye = lax.broadcasted_iota(jnp.int32, (16, 16), 0) == lax.broadcasted_iota(jnp.int32, (16, 16), 1)

    def column(row):
        spread_row = jnp.where(eye, jnp.broadcast_to(row, (16, 16)), 0.0)
        return jnp.broadcast_to(jnp.sum(spread_row, axis=1, keepdims=True), (16, 128))

    coup = [column(coup_v[i:i + 1, :]) for i in range(4)]
    diagonal = column(kappa_v[...]) + (coup[0] + coup[1] + coup[2] + coup[3])
    table = jnp.concatenate([diagonal] + coup, axis=1)
    high = table.astype(BF16)
    rest = table - high.astype(F32)
    mid = rest.astype(BF16)
    tail = (rest - mid.astype(F32)).astype(BF16)
    table3 = jnp.concatenate([high, mid, tail], axis=0)
    level = lax.broadcasted_iota(jnp.int32, (48, 128), 0) % 16
    for k in range(8):
        onehot = (jnp.broadcast_to(cls[k:k + 1, :], (48, 128)) == level).astype(F32).astype(BF16)
        rows = lax.dot_general(onehot, table3, (((0,), (0,)), ((), ())), preferred_element_type=F32)
        for q in range(5):
            coef[k, q] = rows[:80, q * 128:(q + 1) * 128]

    c_row = px * 8 + 2 * f - 4
    col80 = lax.broadcasted_iota(jnp.int32, (80, 128), 0) + (py * 64 - 8)
    col_ok = (col80 >= 0) & (col80 < npy * 64)

    def fill(i, carry):
        row_ok = (c_row + i >= 0) & (c_row + i < npx * 8)
        va[i] = jnp.where(col_ok & row_ok, ext[2 * f + i], 0.0)
        return carry

    lax.fori_loop(0, 10, fill, 0)

    src, dst = va, vb
    for sweep in range(SWEEPS):
        def row_step(i, carry, src=src, dst=dst):
            center = src[i]
            beside = coef[i - 1, 1] * src[i - 1] + coef[i - 1, 2] * src[i + 1]
            beside = beside + coef[i - 1, 3] * rolled(center, 1, 0) + coef[i - 1, 4] * rolled(center, -1, 0)
            dst[i] = coef[i - 1, 0] * center - beside
            return carry

        lax.fori_loop(1 + sweep, 9 - sweep, row_step, 0)
        src, dst = dst, src
    fown[...] = PRIOR_WEIGHT * src[4:6, 8:72, :]

    ac_copies = []
    for i, a in enumerate((0, 1, 3, 2)):
        for d in far_y[::-1]:
            if (a, d) in a_copies:
                a_copies[a, d].wait_recv()
        column_x = wf.at[c, :, :, (x + NX_CHIP - a) % NX_CHIP]
        copy = remote(column_x, column_x, acsem, i, partner)
        copy.start()
        ac_copies.append(copy)

    t_copy.wait_recv()
    other = wtin[...]
    half0 = jnp.where(c == 0, w_own, other)
    half1 = jnp.where(c == 0, other, w_own)
    half0 = jnp.where(c == 0, half0[0:4], half0[4:8])
    half1 = jnp.where(c == 0, half1[0:4], half1[4:8])
    wout[pl.ds(0, 4, stride=2), :] = jnp.where(lo4, half0, rolled(half1, 64, 1))
    wout[pl.ds(1, 4, stride=2), :] = jnp.where(lo4, rolled(half0, 64, 1), half1)

    for copy in ac_copies:
        copy.wait_recv()
    weights = jnp.concatenate(
        [wf.at[h].reshape(512, 128)[...] for h in range(2)], axis=1
    )

    lo64 = lax.broadcasted_iota(jnp.int32, (64, 128), 1) < 64
    steps = (3, 2, 1, 0)
    r_copies, totals = [[], []], []
    for h in range(2):
        kq = []
        for d in steps:
            rows = pl.ds(pl.multiple_of((f + d) % NF * 256 + h * 128, 128), 128)
            kq.append(jnp.concatenate([kscr.at[lb].reshape(1024, 128)[rows, :] for lb in range(4)], axis=1))
        both = jnp.dot(jnp.concatenate(kq, axis=0), weights, preferred_element_type=F32)
        g[h, 0] = both[:, :128]
        g[h, 1] = both[:, 128:]
        for i, d in enumerate(steps):
            e0, o0, e1, o1 = [
                g.at[h, half][pl.ds(i * 128 + odd_row, 64, stride=2), :] for half in range(2) for odd_row in range(2)
            ]
            grad = jnp.where(lo64, e0, o1) + rolled(jnp.where(lo64, e1, o0), 64, 1)
            if d:
                fsend[d - 1, h] = grad.astype(BF16)
                copy = remote(fsend.at[d - 1, h], fin.at[d - 1, h], rsem, (d - 1) * 2 + h, f_peers[d - 1])
                copy.start()
                r_copies[h].append(copy)
            else:
                totals.append(grad + fown[h])
    g_copies, own = [], []
    for h in range(2):
        for copy in r_copies[h]:
            copy.wait_recv()
        total = totals[h] + (fin[0, h].astype(F32) + fin[1, h].astype(F32)) + fin[2, h].astype(F32)
        fsum[h] = total.astype(BF16)
        row = gout.at[2 * f + h]
        for d in (3, 2, 1):
            copy = remote(fsum.at[h], row, gsem, (d - 1) * 2 + h, f_peers[d - 1])
            copy.start()
            g_copies.append(copy)
        copy = pltpu.make_async_copy(fsum.at[h], row, lsem.at[10 + h])
        copy.start()
        own.append(copy)
    for copy in g_copies:
        copy.wait_recv()
    for copy in own:
        copy.wait()
    everything = (
        c_copies + [on_copy, n_copy] + x_copies + v_copies + y_copies + h_copies + list(a_copies.values())
        + [t_copy] + ac_copies + r_copies[0] + r_copies[1] + g_copies
    )
    for copy in everything:
        copy.wait_send()


def local(observed, noise_scale, forward_kernel, model_field, classes, kappa_table, coupling_table):
    vmem = lambda shape, dtype=F32: pltpu.VMEM(shape, dtype)
    sems = lambda n: pltpu.SemaphoreType.DMA((2, n))
    weighted, grad = pl.pallas_call(
        kernel,
        name="gauss_newton",
        out_shape=(
            jax.ShapeDtypeStruct((8, 128), F32),
            jax.ShapeDtypeStruct((8, 64, 128), BF16),
        ),
        in_specs=[pl.BlockSpec(memory_space=pltpu.HBM)] * 7,
        out_specs=(pl.BlockSpec(memory_space=pltpu.VMEM), pl.BlockSpec(memory_space=pl.ANY)),
        scratch_shapes=[
            vmem((4, 512, 2, 128), BF16), vmem((16, 80, 128)), vmem((8, 128)), vmem((1, 4)),
            vmem((3, 24, 64), jnp.int32), vmem((1, 16)), vmem((4, 16)),
            vmem((2, 1024, 128)), vmem((2, 16, 4, 8, 128)), vmem((16, 4, 8, 128)), vmem((2, 8, 128)), vmem((2, 8, 128)),
            vmem((3, 16, 8, 128)), vmem((2, 8, 8, 128)), vmem((15, 2, 8, 128)), vmem((8, 128)), vmem((8, 128)),
            vmem((2, 2, 8, 4, 8, 128), BF16), vmem((8, 128)), vmem((8, 128)),
            vmem((2, 2, 512, 128)), vmem((3, 2, 64, 128), BF16), vmem((3, 2, 64, 128), BF16), vmem((2, 64, 128), BF16), vmem((2, 64, 128)),
            vmem((10, 80, 128)), vmem((10, 80, 128)), vmem((8, 5, 80, 128)), vmem((8, 128), jnp.int32),
            pltpu.SemaphoreType.DMA((12,)), sems(4), sems(12), sems(15), sems(1), sems(1), sems(31), sems(4), sems(1),
            sems(6), sems(6), sems(6), pltpu.SemaphoreType.REGULAR,
        ],
        compiler_params=pltpu.CompilerParams(
            collective_id=0, has_side_effects=True, vmem_limit_bytes=48 * 1024 * 1024
        ),
    )(*(pltpu.with_memory_space_constraint(a, pltpu.HBM) for a in (
        forward_kernel.reshape(512, 2, 512),
        model_field,
        observed.reshape(8, 128),
        noise_scale,
        classes,
        kappa_table.reshape(1, 16),
        coupling_table,
    )))
    return weighted.reshape(observed.shape), grad.astype(F32)


def solution(mesh):
    in_specs = (
        P("freq", ("px", "py"), None, None),
        P("freq", ("px", "py")),
        P("freq", "px", "py", None, None),
        P("px", "py", None),
        P("px", "py"),
        P(),
        P(),
    )
    out_specs = (P("freq", ("px", "py"), None, None), P("px", "py", None))
    return jax.shard_map(local, mesh=mesh, in_specs=in_specs, out_specs=out_specs, check_vma=False)
```

```python
import functools

import jax
import jax.numpy as jnp
from jax import lax
from jax.experimental import pallas as pl
from jax.experimental.pallas import tpu as pltpu
from jax.sharding import PartitionSpec as P

SWEEPS = 4
FREEDOM = 4.0
PRIOR_WEIGHT = 0.04
MESH = pl.DeviceIdType.MESH
F32, BF16 = jnp.float32, jnp.bfloat16

NF, NZ, NY_CHIP, NX_CHIP = 4, 2, 8, 4


def rolled(v, shift, axis):
    return pltpu.roll(v, shift % v.shape[axis], axis)


def kernel(
    k_hbm, m_hbm, obs_hbm, noise_hbm, cls_hbm, kappa_hbm, coup_hbm,
    wout, gout,
    kscr, ext, vsend, vrecv, obs_v, noise_v, cls_in, kappa_v, coup_v,
    mx, p, cin, onout, onin, xin, b, yin, zout, zin, wf, wt, wtin,
    g, fsend, fin, fsum, fown, va, vb, coef, cls,
    lsem, csem, xsem, ysem, zsem, osem, aysem, acsem, tsem, rsem, gsem, hsem, ready,
):
    f = lax.axis_index("freq")
    px = lax.axis_index("px")
    py = lax.axis_index("py")
    zh, y = px // NY_CHIP, px % NY_CHIP
    x, c = py // 2, py % 2

    def dev(f=f, zh=zh, y=y, x=x, c=c):
        return {"freq": f, "px": zh * NY_CHIP + y, "py": x * 2 + c}

    partner = dev(c=1 - c)
    x_peers = [dev(x=(x + d) % NX_CHIP) for d in range(1, NX_CHIP)]
    z_peer = dev(zh=1 - zh)
    far_y = (4, 3, 5, 2, 6, 1, 7, 0)
    yz_steps = [(d, e) for e in (1, 0) for d in far_y if (d, e) != (0, 0)]
    yz_peers = [dev(y=(y + d) % NY_CHIP, zh=(zh + e) % NZ) for d, e in yz_steps]
    xy_steps = [(a, d) for d in far_y for a in (2, 1, 3, 0) if (a, d) != (0, 0)]
    xy_peers = [dev(x=(x + a) % NX_CHIP, y=(y + d) % NY_CHIP) for a, d in xy_steps]
    f_peers = [dev(f=(f + d) % NF) for d in range(1, NF)]
    npx, npy = NZ * NY_CHIP, NX_CHIP * 2
    left = {"freq": f, "px": px, "py": (py + npy - 1) % npy}
    right = {"freq": f, "px": px, "py": (py + 1) % npy}

    def load(src, dst, i):
        copy = pltpu.make_async_copy(src, dst, lsem.at[i])
        copy.start()
        return copy

    m_load = load(m_hbm, ext.at[4:12, 8:72], 0)
    k_loads = [load(k_hbm.at[:, :, pl.ds(lb * 128, 128)], kscr.at[lb], 1 + lb) for lb in range(4)]
    small = [
        load(obs_hbm, obs_v, 5), load(noise_hbm, noise_v, 6), load(cls_hbm, cls_in.at[1, 8:16], 7),
        load(kappa_hbm, kappa_v, 8), load(coup_hbm, coup_v, 9),
    ]

    bar = pltpu.get_barrier_semaphore()
    zc = zh * NF + f

    def zdev(k):
        z = (zc + k) % (NZ * NF)
        return dev(f=z % NF, zh=z // NF)

    two_off = [dev(y=(y + k) % NY_CHIP) for k in (2, NY_CHIP - 2)] + [zdev(k) for k in (2, NZ * NF - 2)]
    one_off = [dev(y=(y + k) % NY_CHIP) for k in (1, NY_CHIP - 1)] + [zdev(k) for k in (1, NZ * NF - 1)]
    greeted = [partner, left, right] + x_peers + one_off + two_off
    for peer in greeted:
        pl.semaphore_signal(bar, inc=1, device_id=peer, device_id_type=MESH)

    def remote(src, dst, sems, i, peer):
        return pltpu.make_async_remote_copy(
            src_ref=src, dst_ref=dst, send_sem=sems.at[0, i], recv_sem=sems.at[1, i],
            device_id=peer, device_id_type=MESH,
        )

    lane = lax.broadcasted_iota(jnp.int32, (8, 128), 1)
    sub = lax.broadcasted_iota(jnp.int32, (8, 128), 0)

    m_load.wait()
    m = ext[4:12, 8:72, :].reshape(512, 128)
    low = lax.broadcasted_iota(jnp.int32, (512, 128), 1) < 64
    mr = rolled(m, 64, 1)
    mx.at[0][pl.ds(0, 512, stride=2), :] = jnp.where(low, m, 0.0)
    mx.at[0][pl.ds(1, 512, stride=2), :] = jnp.where(low, 0.0, mr)
    mx.at[1][pl.ds(0, 512, stride=2), :] = jnp.where(low, mr, 0.0)
    mx.at[1][pl.ds(1, 512, stride=2), :] = jnp.where(low, 0.0, m)
    model = jnp.concatenate([mx[0].astype(BF16), mx[1].astype(BF16)], axis=1)

    for copy in small:
        copy.wait()
    even = obs_v[pl.ds(0, 4, stride=2), :]
    odd = obs_v[pl.ds(1, 4, stride=2), :]
    lo4 = lax.broadcasted_iota(jnp.int32, (4, 128), 1) < 64
    mine = (sub // 4) == c
    obs_tiles = []
    for t in (jnp.where(lo4, even, rolled(odd, 64, 1)), jnp.where(lo4, rolled(even, 64, 1), odd)):
        obs_tiles.append(jnp.where(mine, jnp.concatenate([t, t], axis=0), 0.0))
    nrow = jnp.broadcast_to(noise_v[...], (8, 4))
    pick = lax.broadcasted_iota(jnp.int32, (8, 4), 1) == lax.broadcasted_iota(jnp.int32, (8, 4), 0) - c * 4
    noise_tile = jnp.broadcast_to(jnp.sum(jnp.where(pick, nrow, 0.0), axis=1, keepdims=True), (8, 128))
    onout[0] = jnp.where(c == 0, obs_tiles[1], obs_tiles[0])
    onout[1] = noise_tile
    obs_own = jnp.where(c == 0, obs_tiles[0], obs_tiles[1])

    vsend[...] = ext[pl.ds(jnp.where(f < 2, 8, 4), 4), 8:72, :].astype(BF16)

    c_copies = []
    for lb in range(4):
        k_loads[lb].wait()
        kv = kscr.at[lb].reshape(1024, 128)[...]
        part = lax.dot_general(kv, model, (((0,), (0,)), ((), ())), preferred_element_type=F32)
        rows = pl.ds(lb * 4, 4)
        p[0, rows] = part[:, :128].reshape(4, 4, 8, 128)
        p[1, rows] = part[:, 128:].reshape(4, 4, 8, 128)
        if lb == 0:
            pl.semaphore_wait(bar, len(greeted))
            for peer in two_off:
                pl.semaphore_signal(ready.at[0], inc=1, device_id=peer, device_id_type=MESH)
        copy = remote(p.at[1 - c, rows], cin.at[rows], csem, lb, partner)
        copy.start()
        c_copies.append(copy)
    on_copy = remote(onout, onin, osem, 0, partner)
    on_copy.start()

    upper = f < 2
    dst_row = jnp.where(upper, 0, 12)
    crosses = (y == jnp.where(upper, NY_CHIP - 1, 0))
    v_peer = {"freq": f, "px": (px + jnp.where(upper, 1, npx - 1)) % npx, "py": py}
    v_copies = [
        remote(vsend, vrecv, hsem, 0, v_peer),
        remote(
            cls_in.at[1, 8:16], cls_in.at[1, pl.ds(pl.multiple_of(jnp.where(upper, 0, 16), 8), 8)],
            hsem, 1, v_peer,
        ),
    ]

    def send_edges():
        for copy in v_copies:
            copy.start()

    pl.when(jnp.logical_not(crosses))(send_edges)

    x_copies = {}
    for lb in range(4):
        rows = pl.ds(lb * 4, 4)
        c_copies[lb].wait_recv()
        p[c, rows] = p[c, rows] + cin[rows]
        for d in (2, 1, 3):
            copy = remote(
                p.at[c, rows, (x + d) % NX_CHIP], xin.at[d - 1, rows], xsem, (d - 1) * 4 + lb, x_peers[d - 1]
            )
            copy.start()
            x_copies[d, lb] = copy

    pl.semaphore_wait(ready.at[0], len(two_off))
    pl.semaphore_signal(ready.at[1], inc=1, device_id=z_peer, device_id_type=MESH)
    on_copy.wait_recv()
    zout[...] = noise_tile + onin[1]
    n_copy = remote(zout, zin, zsem, 0, z_peer)
    n_copy.start()
    obs_chip = obs_own + onin[0]
    pl.semaphore_wait(ready.at[1], 1)
    pl.when(crosses)(send_edges)

    y_copies = []
    for zi in range(NZ):
        for (d, lb), copy in x_copies.items():
            if lb // 2 == zi:
                copy.wait_recv()
        half = pl.ds(zi * NY_CHIP, NY_CHIP)
        b[zi] = p[c, half, x] + xin[0, half] + (xin[1, half] + xin[2, half])
        b[zi, y] = b[zi, y] - jnp.where(zh == zi, obs_chip, 0.0)
        for i, (d, e) in enumerate(yz_steps):
            copy = remote(b.at[zi, (y + d) % NY_CHIP], yin.at[i, zi], ysem, i * NZ + zi, yz_peers[i])
            copy.start()
            y_copies.append(copy)

    for copy in v_copies:
        copy.wait_recv()
    ext[pl.ds(dst_row, 4), 8:72, :] = vrecv[...].astype(F32)
    rows10 = pl.ds(2 * f, 10)
    rows16 = pl.ds(pl.multiple_of(jnp.where(upper, 0, 8), 8), 16)
    h_copies = [
        remote(ext.at[rows10, 8:16], ext.at[rows10, 72:80], hsem, 2, left),
        remote(ext.at[rows10, 64:72], ext.at[rows10, 0:8], hsem, 3, right),
        remote(cls_in.at[1, rows16], cls_in.at[2, rows16], hsem, 4, left),
        remote(cls_in.at[1, rows16], cls_in.at[0, rows16], hsem, 5, right),
    ]
    for copy in h_copies:
        copy.start()

    n_copy.wait_recv()
    for copy in y_copies:
        copy.wait_recv()
    terms = [b[:, y]] + [yin[i] for i in range(len(yz_steps))]
    while len(terms) > 1:
        terms = [u + v for u, v in zip(terms[::2], terms[1::2])]

    w_own = jnp.zeros((8, 128), F32)
    for zi in range(NZ):
        misfit = terms[0][zi]
        noise = jnp.where(zh == zi, zout[...], zin[...])
        inverse = 1.0 / (noise * noise)
        square = misfit * misfit
        spread = (square + rolled(square, 64, 1)) * inverse
        weighted = misfit * ((FREEDOM + 2.0) / (FREEDOM + spread) * inverse)
        wf[c, zi, y, x] = weighted.astype(BF16)
        w_own = jnp.where(zh == zi, weighted, w_own)
    wt[...] = w_own

    a_copies = {}
    for i, (a, d) in enumerate(xy_steps):
        copy = remote(wf.at[c, :, y, x], wf.at[c, :, y, x], aysem, i, xy_peers[i])
        copy.start()
        a_copies[a, d] = copy
    t_copy = remote(wt, wtin, tsem, 0, partner)
    t_copy.start()

    for copy in h_copies:
        copy.wait_recv()
    blocks = []
    for blk in range(3):
        rows = [cls_in[blk, 5 + 2 * i: 13 + 2 * i, :] for i in range(NF)]
        v = jnp.where(f == 0, rows[0], jnp.where(f == 1, rows[1], jnp.where(f == 2, rows[2], rows[3])))
        blocks.append(jnp.concatenate([v, v], axis=1))
    here = jnp.where(lane < 8, rolled(blocks[0], 72, 1), jnp.where(lane < 72, rolled(blocks[1], 8, 1), rolled(blocks[2], 72, 1)))
    grow = px * 8 + 2 * f - 3 + sub
    gcol = py * 64 + lane - 8
    ok = (grow >= 0) & (grow < npx * 8) & (gcol >= 0) & (gcol < npy * 64) & (lane < 80)
    cls[...] = jnp.where(ok, here, -1)

    eye = lax.broadcasted_iota(jnp.int32, (16, 16), 0) == lax.broadcasted_iota(jnp.int32, (16, 16), 1)

    def column(row):
        spread_row = jnp.where(eye, jnp.broadcast_to(row, (16, 16)), 0.0)
        return jnp.broadcast_to(jnp.sum(spread_row, axis=1, keepdims=True), (16, 128))

    coup = [column(coup_v[i:i + 1, :]) for i in range(4)]
    diagonal = column(kappa_v[...]) + (coup[0] + coup[1] + coup[2] + coup[3])
    table = jnp.concatenate([diagonal] + coup, axis=1)
    high = table.astype(BF16)
    rest = table - high.astype(F32)
    mid = rest.astype(BF16)
    tail = (rest - mid.astype(F32)).astype(BF16)
    table3 = jnp.concatenate([high, mid, tail], axis=0)
    level = lax.broadcasted_iota(jnp.int32, (48, 128), 0) % 16
    for k in range(8):
        onehot = (jnp.broadcast_to(cls[k:k + 1, :], (48, 128)) == level).astype(F32).astype(BF16)
        rows = lax.dot_general(onehot, table3, (((0,), (0,)), ((), ())), preferred_element_type=F32)
        for q in range(5):
            coef[k, q] = rows[:80, q * 128:(q + 1) * 128]

    c_row = px * 8 + 2 * f - 4
    col80 = lax.broadcasted_iota(jnp.int32, (80, 128), 0) + (py * 64 - 8)
    col_ok = (col80 >= 0) & (col80 < npy * 64)

    def fill(i, carry):
        row_ok = (c_row + i >= 0) & (c_row + i < npx * 8)
        va[i] = jnp.where(col_ok & row_ok, ext[2 * f + i], 0.0)
        return carry

    lax.fori_loop(0, 10, fill, 0)

    src, dst = va, vb
    for sweep in range(SWEEPS):
        def row_step(i, carry, src=src, dst=dst):
            center = src[i]
            beside = coef[i - 1, 1] * src[i - 1] + coef[i - 1, 2] * src[i + 1]
            beside = beside + coef[i - 1, 3] * rolled(center, 1, 0) + coef[i - 1, 4] * rolled(center, -1, 0)
            dst[i] = coef[i - 1, 0] * center - beside
            return carry

        lax.fori_loop(1 + sweep, 9 - sweep, row_step, 0)
        src, dst = dst, src
    fown[...] = PRIOR_WEIGHT * src[4:6, 8:72, :]

    ac_copies = []
    for i, a in enumerate((0, 1, 3, 2)):
        for d in far_y[::-1]:
            if (a, d) in a_copies:
                a_copies[a, d].wait_recv()
        column_x = wf.at[c, :, :, (x + NX_CHIP - a) % NX_CHIP]
        copy = remote(column_x, column_x, acsem, i, partner)
        copy.start()
        ac_copies.append(copy)

    t_copy.wait_recv()
    other = wtin[...]
    half0 = jnp.where(c == 0, w_own, other)
    half1 = jnp.where(c == 0, other, w_own)
    half0 = jnp.where(c == 0, half0[0:4], half0[4:8])
    half1 = jnp.where(c == 0, half1[0:4], half1[4:8])
    wout[pl.ds(0, 4, stride=2), :] = jnp.where(lo4, half0, rolled(half1, 64, 1))
    wout[pl.ds(1, 4, stride=2), :] = jnp.where(lo4, rolled(half0, 64, 1), half1)

    for copy in ac_copies:
        copy.wait_recv()
    weights = jnp.concatenate(
        [wf.at[h].reshape(512, 128)[...] for h in range(2)], axis=1
    )

    lo64 = lax.broadcasted_iota(jnp.int32, (64, 128), 1) < 64
    steps = (3, 2, 1, 0)
    r_copies, totals = [[], []], []
    for h in range(2):
        kq = []
        for d in steps:
            rows = pl.ds(pl.multiple_of((f + d) % NF * 256 + h * 128, 128), 128)
            kq.append(jnp.concatenate([kscr.at[lb].reshape(1024, 128)[rows, :] for lb in range(4)], axis=1))
        both = jnp.dot(jnp.concatenate(kq, axis=0), weights, preferred_element_type=F32)
        g[h, 0] = both[:, :128]
        g[h, 1] = both[:, 128:]
        for i, d in enumerate(steps):
            e0, o0, e1, o1 = [
                g.at[h, half][pl.ds(i * 128 + odd_row, 64, stride=2), :] for half in range(2) for odd_row in range(2)
            ]
            grad = jnp.where(lo64, e0, o1) + rolled(jnp.where(lo64, e1, o0), 64, 1)
            if d:
                fsend[d - 1, h] = grad.astype(BF16)
                copy = remote(fsend.at[d - 1, h], fin.at[d - 1, h], rsem, (d - 1) * 2 + h, f_peers[d - 1])
                copy.start()
                r_copies[h].append(copy)
            else:
                totals.append(grad + fown[h])
    g_copies, own = [], []
    for h in range(2):
        for copy in r_copies[h]:
            copy.wait_recv()
        total = totals[h] + (fin[0, h].astype(F32) + fin[1, h].astype(F32)) + fin[2, h].astype(F32)
        fsum[h] = total.astype(BF16)
        row = gout.at[2 * f + h]
        for d in (3, 2, 1):
            copy = remote(fsum.at[h], row, gsem, (d - 1) * 2 + h, f_peers[d - 1])
            copy.start()
            g_copies.append(copy)
        copy = pltpu.make_async_copy(fsum.at[h], row, lsem.at[10 + h])
        copy.start()
        own.append(copy)
    for copy in g_copies:
        copy.wait_recv()
    for copy in own:
        copy.wait()
    everything = (
        c_copies + [on_copy, n_copy] + list(x_copies.values()) + v_copies + y_copies + h_copies + list(a_copies.values())
        + [t_copy] + ac_copies + r_copies[0] + r_copies[1] + g_copies
    )
    for copy in everything:
        copy.wait_send()


def finish(weighted_ref, grad_ref, weighted_out, grad_out):
    weighted_out[...] = weighted_ref[...]
    grad_out[...] = grad_ref[...].astype(F32)


def local(observed, noise_scale, forward_kernel, model_field, classes, kappa_table, coupling_table):
    vmem = lambda shape, dtype=F32: pltpu.VMEM(shape, dtype)
    sems = lambda n: pltpu.SemaphoreType.DMA((2, n))
    weighted, grad = pl.pallas_call(
        kernel,
        name="gauss_newton",
        out_shape=(
            jax.ShapeDtypeStruct((8, 128), F32),
            jax.ShapeDtypeStruct((8, 64, 128), BF16),
        ),
        in_specs=[pl.BlockSpec(memory_space=pltpu.HBM)] * 7,
        out_specs=(pl.BlockSpec(memory_space=pltpu.VMEM), pl.BlockSpec(memory_space=pl.ANY)),
        scratch_shapes=[
            vmem((4, 512, 2, 128), BF16), vmem((16, 80, 128)), vmem((4, 64, 128), BF16), vmem((4, 64, 128), BF16),
            vmem((8, 128)), vmem((1, 4)),
            vmem((3, 24, 64), jnp.int32), vmem((1, 16)), vmem((4, 16)),
            vmem((2, 1024, 128)), vmem((2, 16, 4, 8, 128)), vmem((16, 4, 8, 128)), vmem((2, 8, 128)), vmem((2, 8, 128)),
            vmem((3, 16, 8, 128)), vmem((2, 8, 8, 128)), vmem((15, 2, 8, 128)), vmem((8, 128)), vmem((8, 128)),
            vmem((2, 2, 8, 4, 8, 128), BF16), vmem((8, 128)), vmem((8, 128)),
            vmem((2, 2, 512, 128)), vmem((3, 2, 64, 128), BF16), vmem((3, 2, 64, 128), BF16), vmem((2, 64, 128), BF16), vmem((2, 64, 128)),
            vmem((10, 80, 128)), vmem((10, 80, 128)), vmem((8, 5, 80, 128)), vmem((8, 128), jnp.int32),
            pltpu.SemaphoreType.DMA((12,)), sems(4), sems(12), sems(30), sems(1), sems(1), sems(31), sems(4), sems(1),
            sems(6), sems(6), sems(6), pltpu.SemaphoreType.REGULAR((2,)),
        ],
        compiler_params=pltpu.CompilerParams(
            collective_id=0, has_side_effects=True, vmem_limit_bytes=48 * 1024 * 1024
        ),
    )(*(pltpu.with_memory_space_constraint(a, pltpu.HBM) for a in (
        forward_kernel.reshape(512, 2, 512),
        model_field,
        observed.reshape(8, 128),
        noise_scale,
        classes,
        kappa_table.reshape(1, 16),
        coupling_table,
    )))
    weighted, grad = pl.pallas_call(
        finish,
        name="finish",
        compiler_params=pltpu.CompilerParams(vmem_limit_bytes=4 * 1024 * 1024),
        out_shape=(jax.ShapeDtypeStruct(weighted.shape, F32), jax.ShapeDtypeStruct(grad.shape, F32)),
    )(weighted, grad)
    return weighted.reshape(observed.shape), grad


def solution(mesh):
    in_specs = (
        P("freq", ("px", "py"), None, None),
        P("freq", ("px", "py")),
        P("freq", "px", "py", None, None),
        P("px", "py", None),
        P("px", "py"),
        P(),
        P(),
    )
    out_specs = (P("freq", ("px", "py"), None, None), P("px", "py", None))
    return jax.shard_map(local, mesh=mesh, in_specs=in_specs, out_specs=out_specs, check_vma=False)
```

```python
import functools

import jax
import jax.numpy as jnp
from jax import lax
from jax.experimental import pallas as pl
from jax.experimental.pallas import tpu as pltpu
from jax.sharding import PartitionSpec as P

SWEEPS = 4
FREEDOM = 4.0
PRIOR_WEIGHT = 0.04
MESH = pl.DeviceIdType.MESH
F32, BF16 = jnp.float32, jnp.bfloat16

NF, NZ, NY_CHIP, NX_CHIP = 4, 2, 8, 4


def rolled(v, shift, axis):
    return pltpu.roll(v, shift % v.shape[axis], axis)


def kernel(
    k_hbm, m_hbm, obs_hbm, noise_hbm, cls_hbm, kappa_hbm, coup_hbm,
    wout, gout,
    kscr, kother, ext, vsend, vrecv, obs_v, noise_v, cls_in, kappa_v, coup_v,
    mx, p, cin, onout, onin, xin, b, yin, zout, zin, wf, wt, wtin, pout, pin,
    g, fsend, fin, fsum, fown, va, vb, coef, cls,
    lsem, csem, xsem, ysem, zsem, osem, aysem, ksem, psem, tsem, rsem, gsem, hsem, ready,
):
    f = lax.axis_index("freq")
    px = lax.axis_index("px")
    py = lax.axis_index("py")
    zh, y = px // NY_CHIP, px % NY_CHIP
    x, c = py // 2, py % 2

    def dev(f=f, zh=zh, y=y, x=x, c=c):
        return {"freq": f, "px": zh * NY_CHIP + y, "py": x * 2 + c}

    partner = dev(c=1 - c)
    x_peers = [dev(x=(x + d) % NX_CHIP) for d in range(1, NX_CHIP)]
    z_peer = dev(zh=1 - zh)
    far_y = (4, 3, 5, 2, 6, 1, 7, 0)
    yz_steps = [(d, e) for e in (1, 0) for d in far_y if (d, e) != (0, 0)]
    yz_peers = [dev(y=(y + d) % NY_CHIP, zh=(zh + e) % NZ) for d, e in yz_steps]
    xy_steps = [(a, d) for d in far_y for a in (2, 1, 3, 0) if (a, d) != (0, 0)]
    xy_peers = [dev(x=(x + a) % NX_CHIP, y=(y + d) % NY_CHIP) for a, d in xy_steps]
    f_peers = [dev(f=(f + d) % NF) for d in range(1, NF)]
    npx, npy = NZ * NY_CHIP, NX_CHIP * 2
    left = {"freq": f, "px": px, "py": (py + npy - 1) % npy}
    right = {"freq": f, "px": px, "py": (py + 1) % npy}

    def load(src, dst, i):
        copy = pltpu.make_async_copy(src, dst, lsem.at[i])
        copy.start()
        return copy

    m_load = load(m_hbm, ext.at[4:12, 8:72], 0)
    k_loads = [load(k_hbm.at[:, :, pl.ds(lb * 128, 128)], kscr.at[lb], 1 + lb) for lb in range(4)]
    small = [
        load(obs_hbm, obs_v, 5), load(noise_hbm, noise_v, 6), load(cls_hbm, cls_in.at[1, 8:16], 7),
        load(kappa_hbm, kappa_v, 8), load(coup_hbm, coup_v, 9),
    ]

    bar = pltpu.get_barrier_semaphore()
    zc = zh * NF + f

    def zdev(k):
        z = (zc + k) % (NZ * NF)
        return dev(f=z % NF, zh=z // NF)

    two_off = [dev(y=(y + k) % NY_CHIP) for k in (2, NY_CHIP - 2)] + [zdev(k) for k in (2, NZ * NF - 2)]
    one_off = [dev(y=(y + k) % NY_CHIP) for k in (1, NY_CHIP - 1)] + [zdev(k) for k in (1, NZ * NF - 1)]
    greeted = [partner, left, right] + x_peers + one_off + two_off
    for peer in greeted:
        pl.semaphore_signal(bar, inc=1, device_id=peer, device_id_type=MESH)

    def remote(src, dst, sems, i, peer):
        return pltpu.make_async_remote_copy(
            src_ref=src, dst_ref=dst, send_sem=sems.at[0, i], recv_sem=sems.at[1, i],
            device_id=peer, device_id_type=MESH,
        )

    lane = lax.broadcasted_iota(jnp.int32, (8, 128), 1)
    sub = lax.broadcasted_iota(jnp.int32, (8, 128), 0)

    m_load.wait()
    m = ext[4:12, 8:72, :].reshape(512, 128)
    low = lax.broadcasted_iota(jnp.int32, (512, 128), 1) < 64
    mr = rolled(m, 64, 1)
    mx.at[0][pl.ds(0, 512, stride=2), :] = jnp.where(low, m, 0.0)
    mx.at[0][pl.ds(1, 512, stride=2), :] = jnp.where(low, 0.0, mr)
    mx.at[1][pl.ds(0, 512, stride=2), :] = jnp.where(low, mr, 0.0)
    mx.at[1][pl.ds(1, 512, stride=2), :] = jnp.where(low, 0.0, m)
    model = jnp.concatenate([mx[0].astype(BF16), mx[1].astype(BF16)], axis=1)

    for copy in small:
        copy.wait()
    even = obs_v[pl.ds(0, 4, stride=2), :]
    odd = obs_v[pl.ds(1, 4, stride=2), :]
    lo4 = lax.broadcasted_iota(jnp.int32, (4, 128), 1) < 64
    mine = (sub // 4) == c
    obs_tiles = []
    for t in (jnp.where(lo4, even, rolled(odd, 64, 1)), jnp.where(lo4, rolled(even, 64, 1), odd)):
        obs_tiles.append(jnp.where(mine, jnp.concatenate([t, t], axis=0), 0.0))
    nrow = jnp.broadcast_to(noise_v[...], (8, 4))
    pick = lax.broadcasted_iota(jnp.int32, (8, 4), 1) == lax.broadcasted_iota(jnp.int32, (8, 4), 0) - c * 4
    noise_tile = jnp.broadcast_to(jnp.sum(jnp.where(pick, nrow, 0.0), axis=1, keepdims=True), (8, 128))
    onout[0] = jnp.where(c == 0, obs_tiles[1], obs_tiles[0])
    onout[1] = noise_tile
    obs_own = jnp.where(c == 0, obs_tiles[0], obs_tiles[1])

    vsend[...] = ext[pl.ds(jnp.where(f < 2, 8, 4), 4), 8:72, :].astype(BF16)

    c_copies = []
    for lb in range(4):
        k_loads[lb].wait()
        kv = kscr.at[lb].reshape(1024, 128)[...]
        part = lax.dot_general(kv, model, (((0,), (0,)), ((), ())), preferred_element_type=F32)
        rows = pl.ds(lb * 4, 4)
        p[0, rows] = part[:, :128].reshape(4, 4, 8, 128)
        p[1, rows] = part[:, 128:].reshape(4, 4, 8, 128)
        if lb == 0:
            pl.semaphore_wait(bar, len(greeted))
            for peer in two_off:
                pl.semaphore_signal(ready.at[0], inc=1, device_id=peer, device_id_type=MESH)
        copy = remote(p.at[1 - c, rows], cin.at[rows], csem, lb, partner)
        copy.start()
        c_copies.append(copy)
    on_copy = remote(onout, onin, osem, 0, partner)
    on_copy.start()

    upper = f < 2
    dst_row = jnp.where(upper, 0, 12)
    crosses = (y == jnp.where(upper, NY_CHIP - 1, 0))
    v_peer = {"freq": f, "px": (px + jnp.where(upper, 1, npx - 1)) % npx, "py": py}
    v_copies = [
        remote(vsend, vrecv, hsem, 0, v_peer),
        remote(
            cls_in.at[1, 8:16], cls_in.at[1, pl.ds(pl.multiple_of(jnp.where(upper, 0, 16), 8), 8)],
            hsem, 1, v_peer,
        ),
    ]

    def send_edges():
        for copy in v_copies:
            copy.start()

    pl.when(jnp.logical_not(crosses))(send_edges)

    x_copies = {}
    for lb in range(4):
        rows = pl.ds(lb * 4, 4)
        c_copies[lb].wait_recv()
        p[c, rows] = p[c, rows] + cin[rows]
        for d in (2, 1, 3):
            copy = remote(
                p.at[c, rows, (x + d) % NX_CHIP], xin.at[d - 1, rows], xsem, (d - 1) * 4 + lb, x_peers[d - 1]
            )
            copy.start()
            x_copies[d, lb] = copy

    pl.semaphore_wait(ready.at[0], len(two_off))
    pl.semaphore_signal(ready.at[1], inc=1, device_id=z_peer, device_id_type=MESH)
    on_copy.wait_recv()
    zout[...] = noise_tile + onin[1]
    n_copy = remote(zout, zin, zsem, 0, z_peer)
    n_copy.start()
    obs_chip = obs_own + onin[0]
    pl.semaphore_wait(ready.at[1], 1)
    pl.when(crosses)(send_edges)

    y_copies = []
    for zi in range(NZ):
        for (d, lb), copy in x_copies.items():
            if lb // 2 == zi:
                copy.wait_recv()
        half = pl.ds(zi * NY_CHIP, NY_CHIP)
        b[zi] = p[c, half, x] + xin[0, half] + (xin[1, half] + xin[2, half])
        b[zi, y] = b[zi, y] - jnp.where(zh == zi, obs_chip, 0.0)
        for i, (d, e) in enumerate(yz_steps):
            copy = remote(b.at[zi, (y + d) % NY_CHIP], yin.at[i, zi], ysem, i * NZ + zi, yz_peers[i])
            copy.start()
            y_copies.append(copy)

    for copy in v_copies:
        copy.wait_recv()
    ext[pl.ds(dst_row, 4), 8:72, :] = vrecv[...].astype(F32)
    rows10 = pl.ds(2 * f, 10)
    rows16 = pl.ds(pl.multiple_of(jnp.where(upper, 0, 8), 8), 16)
    h_copies = [
        remote(ext.at[rows10, 8:16], ext.at[rows10, 72:80], hsem, 2, left),
        remote(ext.at[rows10, 64:72], ext.at[rows10, 0:8], hsem, 3, right),
        remote(cls_in.at[1, rows16], cls_in.at[2, rows16], hsem, 4, left),
        remote(cls_in.at[1, rows16], cls_in.at[0, rows16], hsem, 5, right),
    ]
    for copy in h_copies:
        copy.start()

    k_copy = remote(kscr, kother, ksem, 0, partner)
    k_copy.start()

    n_copy.wait_recv()
    for copy in y_copies:
        copy.wait_recv()
    terms = [b[:, y]] + [yin[i] for i in range(len(yz_steps))]
    while len(terms) > 1:
        terms = [u + v for u, v in zip(terms[::2], terms[1::2])]

    w_own = jnp.zeros((8, 128), F32)
    for zi in range(NZ):
        misfit = terms[0][zi]
        noise = jnp.where(zh == zi, zout[...], zin[...])
        inverse = 1.0 / (noise * noise)
        square = misfit * misfit
        spread = (square + rolled(square, 64, 1)) * inverse
        weighted = misfit * ((FREEDOM + 2.0) / (FREEDOM + spread) * inverse)
        wf[zi, y, x] = weighted.astype(BF16)
        w_own = jnp.where(zh == zi, weighted, w_own)
    wt[...] = w_own

    a_copies = {}
    for i, (a, d) in enumerate(xy_steps):
        copy = remote(wf.at[:, y, x], wf.at[:, y, x], aysem, i, xy_peers[i])
        copy.start()
        a_copies[a, d] = copy
    t_copy = remote(wt, wtin, tsem, 0, partner)
    t_copy.start()

    for copy in h_copies:
        copy.wait_recv()
    blocks = []
    for blk in range(3):
        rows = [cls_in[blk, 5 + 2 * i: 13 + 2 * i, :] for i in range(NF)]
        v = jnp.where(f == 0, rows[0], jnp.where(f == 1, rows[1], jnp.where(f == 2, rows[2], rows[3])))
        blocks.append(jnp.concatenate([v, v], axis=1))
    here = jnp.where(lane < 8, rolled(blocks[0], 72, 1), jnp.where(lane < 72, rolled(blocks[1], 8, 1), rolled(blocks[2], 72, 1)))
    grow = px * 8 + 2 * f - 3 + sub
    gcol = py * 64 + lane - 8
    ok = (grow >= 0) & (grow < npx * 8) & (gcol >= 0) & (gcol < npy * 64) & (lane < 80)
    cls[...] = jnp.where(ok, here, -1)

    eye = lax.broadcasted_iota(jnp.int32, (16, 16), 0) == lax.broadcasted_iota(jnp.int32, (16, 16), 1)

    def column(row):
        spread_row = jnp.where(eye, jnp.broadcast_to(row, (16, 16)), 0.0)
        return jnp.broadcast_to(jnp.sum(spread_row, axis=1, keepdims=True), (16, 128))

    coup = [column(coup_v[i:i + 1, :]) for i in range(4)]
    diagonal = column(kappa_v[...]) + (coup[0] + coup[1] + coup[2] + coup[3])
    table = jnp.concatenate([diagonal] + coup, axis=1)
    high = table.astype(BF16)
    rest = table - high.astype(F32)
    mid = rest.astype(BF16)
    tail = (rest - mid.astype(F32)).astype(BF16)
    table3 = jnp.concatenate([high, mid, tail], axis=0)
    level = lax.broadcasted_iota(jnp.int32, (48, 128), 0) % 16
    for k in range(8):
        onehot = (jnp.broadcast_to(cls[k:k + 1, :], (48, 128)) == level).astype(F32).astype(BF16)
        rows = lax.dot_general(onehot, table3, (((0,), (0,)), ((), ())), preferred_element_type=F32)
        for q in range(5):
            coef[k, q] = rows[:80, q * 128:(q + 1) * 128]

    c_row = px * 8 + 2 * f - 4
    col80 = lax.broadcasted_iota(jnp.int32, (80, 128), 0) + (py * 64 - 8)
    col_ok = (col80 >= 0) & (col80 < npy * 64)

    def fill(i, carry):
        row_ok = (c_row + i >= 0) & (c_row + i < npx * 8)
        va[i] = jnp.where(col_ok & row_ok, ext[2 * f + i], 0.0)
        return carry

    lax.fori_loop(0, 10, fill, 0)

    src, dst = va, vb
    for sweep in range(SWEEPS):
        def row_step(i, carry, src=src, dst=dst):
            center = src[i]
            beside = coef[i - 1, 1] * src[i - 1] + coef[i - 1, 2] * src[i + 1]
            beside = beside + coef[i - 1, 3] * rolled(center, 1, 0) + coef[i - 1, 4] * rolled(center, -1, 0)
            dst[i] = coef[i - 1, 0] * center - beside
            return carry

        lax.fori_loop(1 + sweep, 9 - sweep, row_step, 0)
        src, dst = dst, src
    lo32 = lax.broadcasted_iota(jnp.int32, (32, 128), 1) < 64

    def packed(lo_half):
        return jnp.where(lo32, lo_half[:32], rolled(lo_half[32:], 64, 1))

    for h in range(2):
        prior = PRIOR_WEIGHT * src[4 + h, 8:72, :]
        turned = rolled(prior, 64, 1)
        fown[h] = packed(jnp.where(c == 0, prior, turned))
        pout[h] = packed(jnp.where(c == 0, turned, prior))
    p_copy = remote(pout, pin, psem, 0, partner)
    p_copy.start()

    t_copy.wait_recv()
    other = wtin[...]
    half0 = jnp.where(c == 0, w_own, other)
    half1 = jnp.where(c == 0, other, w_own)
    half0 = jnp.where(c == 0, half0[0:4], half0[4:8])
    half1 = jnp.where(c == 0, half1[0:4], half1[4:8])
    wout[pl.ds(0, 4, stride=2), :] = jnp.where(lo4, half0, rolled(half1, 64, 1))
    wout[pl.ds(1, 4, stride=2), :] = jnp.where(lo4, rolled(half0, 64, 1), half1)

    k_copy.wait_recv()
    p_copy.wait_recv()
    for copy in a_copies.values():
        copy.wait_recv()
    weights = wf.reshape(512, 128)[...]

    r_copies, totals = [[], []], []
    for h in range(2):
        kq = []
        for d in (3, 2, 1, 0):
            rows = pl.ds(pl.multiple_of((f + d) % NF * 256 + h * 128, 128), 128)
            kq += [
                jnp.concatenate([k.at[lb].reshape(1024, 128)[rows, :] for lb in range(4)], axis=1)
                for k in (kscr, kother)
            ]
        g[h] = jnp.dot(jnp.concatenate(kq, axis=0), weights, preferred_element_type=F32).reshape(4, 256, 128)
        for d in (3, 2, 1, 0):
            grads = []
            for k in range(2):
                e, o = [g.at[h, 3 - d][pl.ds(k * 128 + odd_row, 64, stride=2), :] for odd_row in range(2)]
                grads.append(packed(e + rolled(o, 64, 1)))
            grad = jnp.concatenate(grads, axis=0)
            if d:
                fsend[d - 1, h] = grad.astype(BF16)
                copy = remote(fsend.at[d - 1, h], fin.at[d - 1, h], rsem, (d - 1) * 2 + h, f_peers[d - 1])
                copy.start()
                r_copies[h].append(copy)
            else:
                totals.append(grad + jnp.concatenate([fown[h], pin[h]], axis=0))
    g_copies, own = [], []
    for h in range(2):
        for copy in r_copies[h]:
            copy.wait_recv()
        total = totals[h] + (fin[0, h].astype(F32) + fin[1, h].astype(F32)) + fin[2, h].astype(F32)
        fsum[h] = total.astype(BF16).reshape(2, 32, 128)
        row = gout.at[c, 2 * f + h]
        for d in (3, 2, 1, 0):
            for k in range(2):
                if (d, k) != (0, 0):
                    peer = dev(f=(f + d) % NF, c=(c + k) % 2)
                    copy = remote(fsum.at[h, k], row, gsem, (d * 2 + k) * 2 + h, peer)
                    copy.start()
                    g_copies.append(copy)
        copy = pltpu.make_async_copy(fsum.at[h, 0], row, lsem.at[10 + h])
        copy.start()
        own.append(copy)
    for copy in g_copies:
        copy.wait_recv()
    for copy in own:
        copy.wait()
    everything = (
        c_copies + [on_copy, n_copy] + list(x_copies.values()) + v_copies + y_copies + h_copies + list(a_copies.values())
        + [t_copy, k_copy, p_copy] + r_copies[0] + r_copies[1] + g_copies
    )
    for copy in everything:
        copy.wait_send()


def finish(weighted_ref, grad_ref, weighted_out, grad_out):
    weighted_out[...] = weighted_ref[...]
    first, second = grad_ref[0].astype(F32), grad_ref[1].astype(F32)
    low = lax.broadcasted_iota(jnp.int32, first.shape, 2) < 64
    grad_out[:, :32] = jnp.where(low, first, rolled(second, 64, 2))
    grad_out[:, 32:] = jnp.where(low, rolled(first, 64, 2), second)


def local(observed, noise_scale, forward_kernel, model_field, classes, kappa_table, coupling_table):
    vmem = lambda shape, dtype=F32: pltpu.VMEM(shape, dtype)
    sems = lambda n: pltpu.SemaphoreType.DMA((2, n))
    weighted, grad = pl.pallas_call(
        kernel,
        name="gauss_newton",
        out_shape=(
            jax.ShapeDtypeStruct((8, 128), F32),
            jax.ShapeDtypeStruct((2, 8, 32, 128), BF16),
        ),
        in_specs=[pl.BlockSpec(memory_space=pltpu.HBM)] * 7,
        out_specs=(pl.BlockSpec(memory_space=pltpu.VMEM), pl.BlockSpec(memory_space=pl.ANY)),
        scratch_shapes=[
            vmem((4, 512, 2, 128), BF16), vmem((4, 512, 2, 128), BF16), vmem((16, 80, 128)), vmem((4, 64, 128), BF16), vmem((4, 64, 128), BF16),
            vmem((8, 128)), vmem((1, 4)),
            vmem((3, 24, 64), jnp.int32), vmem((1, 16)), vmem((4, 16)),
            vmem((2, 1024, 128)), vmem((2, 16, 4, 8, 128)), vmem((16, 4, 8, 128)), vmem((2, 8, 128)), vmem((2, 8, 128)),
            vmem((3, 16, 8, 128)), vmem((2, 8, 8, 128)), vmem((15, 2, 8, 128)), vmem((8, 128)), vmem((8, 128)),
            vmem((2, 8, 4, 8, 128), BF16), vmem((8, 128)), vmem((8, 128)), vmem((2, 32, 128)), vmem((2, 32, 128)),
            vmem((2, 4, 256, 128)), vmem((3, 2, 64, 128), BF16), vmem((3, 2, 64, 128), BF16), vmem((2, 2, 32, 128), BF16), vmem((2, 32, 128)),
            vmem((10, 80, 128)), vmem((10, 80, 128)), vmem((8, 5, 80, 128)), vmem((8, 128), jnp.int32),
            pltpu.SemaphoreType.DMA((12,)), sems(4), sems(12), sems(30), sems(1), sems(1), sems(31), sems(1), sems(1), sems(1),
            sems(6), sems(16), sems(6), pltpu.SemaphoreType.REGULAR((2,)),
        ],
        compiler_params=pltpu.CompilerParams(
            collective_id=0, has_side_effects=True, vmem_limit_bytes=48 * 1024 * 1024
        ),
    )(*(pltpu.with_memory_space_constraint(a, pltpu.HBM) for a in (
        forward_kernel.reshape(512, 2, 512),
        model_field,
        observed.reshape(8, 128),
        noise_scale,
        classes,
        kappa_table.reshape(1, 16),
        coupling_table,
    )))
    weighted, grad = pl.pallas_call(
        finish,
        name="finish",
        compiler_params=pltpu.CompilerParams(vmem_limit_bytes=4 * 1024 * 1024),
        out_shape=(jax.ShapeDtypeStruct(weighted.shape, F32), jax.ShapeDtypeStruct((8, 64, 128), F32)),
    )(weighted, grad)
    return weighted.reshape(observed.shape), grad


def solution(mesh):
    in_specs = (
        P("freq", ("px", "py"), None, None),
        P("freq", ("px", "py")),
        P("freq", "px", "py", None, None),
        P("px", "py", None),
        P("px", "py"),
        P(),
        P(),
    )
    out_specs = (P("freq", ("px", "py"), None, None), P("px", "py", None))
    return jax.shard_map(local, mesh=mesh, in_specs=in_specs, out_specs=out_specs, check_vma=False)
```
